32 devices in a mesh: tm: 8 (over z, core), mp: 2 (over y), batch: 2 (over x).
Axes of the slice: x: 2, y: 2, z: 4, core: 2. Of those that a mesh axis runs over, the one named last changes fastest.
Arguments:
- frames: bfloat16 [16384, 1024], P(('batch', 'tm')), parts along dimension 0, may hold values from -40 to 40
- norm_gain: float32 [1024], replicated, may hold values from 0.5 to 1.5
- qkv_weight: bfloat16 [3, 1024, 1024], P(None, None, 'mp'), may hold values from -2 to 2
- out_weight: bfloat16 [1024, 1024], P('mp'), may hold values from -0.1875 to 0.1875
- cotangent: bfloat16 [16384, 1024], P(('batch', 'tm')), parts along dimension 0, may hold values from -6 to 6
- pad_mask: int32 [16384], P('batch'), parts along dimension 0, may hold values from 0 to 1, as said below
- utt_lengths: int32 [16], P('batch'), parts along dimension 0, may hold values from 1 to 2048, 8192 in all
Outputs:
- frame_grad: bfloat16 [16384, 1024], P(('batch', 'tm'), 'mp'), parts along dimension 0
- qkv_grad: float32 [6, 1024, 1024], P('batch', 'tm', 'mp'), parts along dimension 0
- out_grad: float32 [2048, 1024], P(('batch', 'mp'), 'tm'), parts along dimension 0
The draws below stay inside these ranges and needn't reach their ends.
There are 2 independent parts, one for each index of `batch`. The reference program is written for one: setup_inputs(seed, part) draws one part's arguments, and reference() takes and returns one part's arrays. A program takes and returns all parts, laid end to end along the dimension named above; an argument that names none is the same for every part. Nothing has to cross between parts.
Inputs may be any that keep to these rules, and one draw needn't show every extreme that they name: `pad_mask`: in each aligned block of 256 frames, the padding frames form the tail of the block, fewer than 128 of them. `utt_lengths`: 8 lengths that sum to 8192; the largest is exactly 2048.
All inputs are finite; a program needn't handle non-finite values.
Results may differ from the reference program's by a relative error of at most 0.012.
The reference program's roundings to bfloat16 on the way count: a program that leaves them out, or rounds other values in their place, can miss the bound.
Values may be sent and summed in bfloat16 or wider, within the bound.
A program may use at most 128 MiB of HBM per device.

```python
import math
import jax
import jax.numpy as jnp
import numpy as np
from jax import lax

D = 1024
HEADS = 8
HS = 128
CH = 32
UTTS = 8
FRAMES = 8192
MAXLEN = 2048


def draw_frames(key, part):
    base = jax.random.normal(key, (FRAMES, D), jnp.float32)
    return jnp.clip(base, -40.0, 40.0).astype(jnp.bfloat16)


def draw_qkv_weight(key, part):
    noise = jax.random.normal(key, (3, D, D), jnp.float32) * D ** (-0.5)
    return jnp.clip(noise, -2.0, 2.0).astype(jnp.bfloat16)


def draw_pad_mask(key, part):
    block_len = 8 * CH
    tails = jax.random.randint(key, (FRAMES // block_len,), 0, block_len // 2)
    positions = jnp.arange(block_len, dtype=jnp.int32)
    keep = (positions[None, :] < block_len - tails[:, None]).astype(jnp.int32)
    return keep.reshape(FRAMES)


def block_scale(own_key, shape, split, least, top_value):
    gain = 1.0
    for axis_at, blocks in split:
        draws = jax.random.uniform(jax.random.fold_in(jax.random.fold_in(own_key, 6), axis_at), (blocks,), jnp.float32, least / len(split), top_value / len(split))
        gain = gain * jnp.repeat(jnp.exp(draws), shape[axis_at] // blocks).reshape((-1,) + (1,) * (len(shape) - 1 - axis_at))
    return gain


def split_up(amount, total, reach, lean):
    portions = [(1 << 20) // math.isqrt(rank ** lean) + 1 for rank in range(2, amount + 1)]
    surplus, counts = total - reach - (amount - 1), [1] * (amount - 1)
    while surplus > 0:
        movable = [i for i in range(amount - 1) if counts[i] < reach]
        pool, remaining = sum([portions[i] for i in movable]), surplus
        for i in movable:
            addition = min(reach - counts[i], max(1, remaining * portions[i] // pool), surplus)
            counts[i] = counts[i] + addition
            surplus = surplus - addition
    return np.array([reach] + counts)


def uneven(rng, number_of, total, reach, skew):
    if number_of == 2:
        one = jax.random.randint(rng, (), max(1, total - reach), min(reach, total - 1) + 1)
        return jnp.stack([one, total - one])
    lengths = jnp.asarray(split_up(number_of, total, reach, skew), jnp.int32)
    couples = (number_of - 1) // 2
    source_of, taker = lengths[1:1 + 2 * couples:2], lengths[2:2 + 2 * couples:2]
    slack = jnp.minimum(source_of - 1, reach - taker)
    moved = jax.random.randint(jax.random.fold_in(rng, 1), (couples,), 0, 1 << 20) % (slack + 1)
    lengths = lengths.at[1:1 + 2 * couples:2].set(source_of - moved).at[2:2 + 2 * couples:2].set(taker + moved)
    return lengths[jax.random.permutation(jax.random.fold_in(rng, 2), number_of)]


def normal_values(stream_key, dims, width, bound, cuts=(), kind=jnp.bfloat16):
    gain = block_scale(stream_key, dims, cuts, -0.22, 0.18) if cuts else 1.0
    array = jax.random.normal(stream_key, dims, jnp.float32) * width * gain
    return jnp.minimum(jnp.maximum(array, -bound), bound).astype(kind)


def setup_inputs(seed: int = 0, part: int = 0) -> dict:
    seeds = jax.random.split(jax.random.key(seed), 8)
    own_keys = jax.random.split(jax.random.fold_in(seeds[7], part), 8)
    frames = draw_frames(jax.random.fold_in(jax.random.fold_in(seeds[7], part), 71), part)
    norm_gain = jnp.clip(1.0 + 0.1 * jax.random.normal(seeds[1], (D,), jnp.float32), 0.5, 1.5)
    qkv_weight = draw_qkv_weight(jax.random.fold_in(seeds[7], 71), part)
    out_weight = normal_values(seeds[3], (D, D), D ** -0.5, 0.1875, ((0, 2),))
    cotangent = normal_values(own_keys[4], (FRAMES, D), 1.0, 6.0, ((0, 8),))
    pad_mask = draw_pad_mask(jax.random.fold_in(jax.random.fold_in(seeds[7], part), 71), part)
    utt_lengths = uneven(own_keys[6], UTTS, FRAMES, MAXLEN, 2).astype(jnp.int32)
    return {"frames": frames, "norm_gain": norm_gain, "qkv_weight": qkv_weight, "out_weight": out_weight, "cotangent": cotangent, "pad_mask": pad_mask, "utt_lengths": utt_lengths}


EPSILON = 1e-05

def layer_norm(frames, norm_gain):
    values = frames.astype(jnp.float32)
    center = values - lax.optimization_barrier(jnp.mean(values, axis=-1, keepdims=True))
    inverse = lax.rsqrt(lax.optimization_barrier(jnp.mean(center * center, axis=-1, keepdims=True)) + EPSILON)
    normal_form = center * inverse
    return (normal_form, inverse, (normal_form * norm_gain).astype(jnp.bfloat16))

def norm_backward(incoming, normal_form, inverse, norm_gain):
    scaled = incoming * norm_gain
    mean_grad = lax.optimization_barrier(jnp.mean(scaled, axis=-1, keepdims=True))
    mean_proj = lax.optimization_barrier(jnp.mean(scaled * normal_form, axis=-1, keepdims=True))
    return inverse * (scaled - mean_grad - normal_form * mean_proj)

def windows(block_rows):
    block_count = block_rows.shape[0] - 2
    return jnp.concatenate([block_rows[:block_count], block_rows[1:block_count + 1], block_rows[2:]], axis=1)

def fold_keys(window):
    block_width = window.shape[1] // 3
    trailing = [(0, 0)] * (window.ndim - 1)
    pieces = [jnp.pad(window[:, offset * block_width:(offset + 1) * block_width], [(offset, 2 - offset)] + trailing) for offset in range(3)]
    return pieces[0] + pieces[1] + pieces[2]

def permitted(query_start, query_count, key_start, key_count, pad_mask, utt_lengths):
    utt_ends = jnp.cumsum(utt_lengths).astype(jnp.int32)
    query_pos = query_start + jnp.arange(query_count, dtype=jnp.int32)
    key_pos = key_start + jnp.arange(key_count, dtype=jnp.int32)

    def segment(positions):
        return lax.optimization_barrier(jnp.sum((utt_ends[None, :] <= positions[:, None]).astype(jnp.int32), axis=1))
    padded = jnp.pad(pad_mask, 2 * CH)
    live_keys = lax.dynamic_slice(padded, (jnp.asarray(key_start + 2 * CH, jnp.int32),), (key_count,))
    query_cells = query_pos.reshape(-1, CH)
    query_seg = segment(query_pos).reshape(-1, CH)
    key_cells = windows(key_pos.reshape(-1, CH))
    key_seg = windows(segment(key_pos).reshape(-1, CH))
    key_live = windows(live_keys.reshape(-1, CH))
    same_utt = query_seg[:, :, None] == key_seg[:, None, :]
    return same_utt & ((key_live[:, None, :] == 1) | (query_cells[:, :, None] == key_cells[:, None, :]))

def product(form, left, right):
    return jnp.einsum(form, left.astype(jnp.float32), right.astype(jnp.float32), precision=lax.Precision.HIGHEST)

def attend(queries, grad_rows, key_blocks, value_blocks, allowed):
    score_scale = HS ** (-0.5)
    key_win = windows(key_blocks)
    value_win = windows(value_blocks)
    scores = product('cihd,cjhd->chij', queries, key_win) * score_scale
    scores = jnp.where(allowed[:, None], scores, -1e+30)
    row_max = lax.optimization_barrier(jnp.max(scores, axis=-1, keepdims=True))
    weights = jnp.exp(scores - row_max)
    attn_probs = weights / lax.optimization_barrier(jnp.sum(weights, axis=-1, keepdims=True))
    rounded = attn_probs.astype(jnp.bfloat16)
    mixed_out = product('chij,cjhd->cihd', rounded, value_win).astype(jnp.bfloat16)
    prob_grad = product('cihd,cjhd->chij', grad_rows, value_win)
    centre = lax.optimization_barrier(jnp.sum(attn_probs * prob_grad, axis=-1, keepdims=True))
    score_grad = (attn_probs * (prob_grad - centre) * score_scale).astype(jnp.bfloat16)
    query_grad = product('chij,cjhd->cihd', score_grad, key_win)
    key_grad = fold_keys(product('chij,cihd->cjhd', score_grad, queries))
    value_grad = fold_keys(product('chij,cihd->cjhd', rounded, grad_rows))
    return (mixed_out, query_grad, key_grad, value_grad)

def reference(frames, norm_gain, qkv_weight, out_weight, cotangent, pad_mask, utt_lengths):
    normal_form, inverse, normed = layer_norm(frames, norm_gain)
    projected = [jnp.dot(normed, qkv_weight[piece], preferred_element_type=jnp.float32).astype(jnp.bfloat16) for piece in range(3)]
    masked = cotangent * pad_mask.astype(jnp.bfloat16)[:, None]
    grad_heads = jnp.dot(masked, out_weight.T, preferred_element_type=jnp.float32).astype(jnp.bfloat16)
    block_count = FRAMES // CH

    def blocks(tensor):
        return tensor.reshape(block_count, CH, HEADS, HS)

    def extend(tensor):
        return jnp.pad(blocks(tensor), ((1, 1), (0, 0), (0, 0), (0, 0)))
    allowed = permitted(0, FRAMES, -CH, FRAMES + 2 * CH, pad_mask, utt_lengths)
    mixed_out, query_grad, key_ext, value_ext = attend(blocks(projected[0]), blocks(grad_heads), extend(projected[1]), extend(projected[2]), allowed)
    all_grads = [gradient.reshape(FRAMES, D).astype(jnp.bfloat16) for gradient in (query_grad, key_ext[1:-1], value_ext[1:-1])]
    qkv_grad = jnp.stack([jnp.dot(normed.T, gradient, preferred_element_type=jnp.float32) for gradient in all_grads])
    out_grad = jnp.dot(mixed_out.reshape(FRAMES, D).T, masked, preferred_element_type=jnp.float32)
    incoming = jnp.dot(all_grads[0], qkv_weight[0].T, preferred_element_type=jnp.float32)
    incoming = incoming + jnp.dot(all_grads[1], qkv_weight[1].T, preferred_element_type=jnp.float32)
    incoming = incoming + jnp.dot(all_grads[2], qkv_weight[2].T, preferred_element_type=jnp.float32)
    frame_grad = norm_backward(incoming, normal_form, inverse, norm_gain).astype(jnp.bfloat16)
    return (frame_grad, qkv_grad, out_grad)
```

```python
import functools

import jax
import jax.numpy as jnp
from jax import lax
from jax.experimental import pallas as pl
from jax.experimental.pallas import tpu as pltpu
from jax.sharding import PartitionSpec as P

HS = 128
CH = 32
HALO = 2 * CH
TILE = 128
EPSILON = 1e-05
VMEM_LIMIT = 60 * 1024 * 1024

BF = jnp.bfloat16
F32 = jnp.float32


def dims(contract_left, contract_right):
    return (((contract_left,), (contract_right,)), ((), ()))


def mm(left, right, contract_left, contract_right):
    return lax.dot_general(
        left, right, dims(contract_left, contract_right), preferred_element_type=F32
    )


def norm_parts(frames):
    values = frames.astype(F32)
    center = values - jnp.mean(values, axis=-1, keepdims=True)
    inverse = lax.rsqrt(jnp.mean(center * center, axis=-1, keepdims=True) + EPSILON)
    return center * inverse, inverse


def project_kernel(x_ref, gain_ref, w_ref, wo_ref, cot_ref, live_ref,
                   normed_ref, masked_ref, q_ref, k_ref, v_ref, g_ref):
    xhat, _ = norm_parts(x_ref[...])
    normed = (xhat * gain_ref[...]).astype(BF)
    normed_ref[...] = normed
    for piece, out in enumerate((q_ref, k_ref, v_ref)):
        out[...] = mm(normed, w_ref[piece], 1, 0).astype(BF)
    masked = jnp.where(live_ref[...] == 1, cot_ref[...].astype(F32), 0.0).astype(BF)
    masked_ref[...] = masked
    g_ref[...] = mm(masked, wo_ref[...], 1, 1).astype(BF)


def project(frames, gain, w, wo, cot, live):
    rows, depth = frames.shape
    cols = w.shape[2]
    step = min(rows, 256)
    row = lambda width: pl.BlockSpec((step, width), lambda i: (i, 0))
    return pl.pallas_call(
        project_kernel,
        name="project",
        grid=(rows // step,),
        in_specs=[
            row(depth),
            pl.BlockSpec((1, depth), lambda i: (0, 0)),
            pl.BlockSpec(w.shape, lambda i: (0, 0, 0)),
            pl.BlockSpec(wo.shape, lambda i: (0, 0)),
            row(depth),
            row(1),
        ],
        out_specs=[row(depth), row(depth)] + [row(cols)] * 4,
        out_shape=[jax.ShapeDtypeStruct((rows, depth), BF)] * 2
        + [jax.ShapeDtypeStruct((rows, cols), BF)] * 4,
        compiler_params=pltpu.CompilerParams(vmem_limit_bytes=VMEM_LIMIT),
        cost_estimate=pl.CostEstimate(
            flops=8 * rows * depth * cols, bytes_accessed=8 * rows * depth, transcendentals=0
        ),
    )(frames, gain, w, wo, cot, live)


def attend_kernel(qseg_ref, kcode_ref, qm, km, vm, gm, qh, kh, vh, gh,
                  o_ref, dq_ref, dk_ref, dv_ref,
                  qe, ke, ve, ge, oe, dqe, dka, dva):
    rows, cols = qm.shape
    edge = TILE + rows
    for ext, main, halo in ((qe, qm, qh), (ke, km, kh), (ve, vm, vh), (ge, gm, gh)):
        ext[0 : TILE - HALO] = jnp.zeros((TILE - HALO, cols), BF)
        ext[TILE - HALO : TILE] = halo[0:HALO]
        ext[TILE:edge] = main[...]
        ext[edge : edge + HALO] = halo[HALO : 2 * HALO]
        ext[edge + HALO : edge + TILE] = jnp.zeros((TILE - HALO, cols), BF)
    dka[...] = jnp.zeros_like(dka)
    dva[...] = jnp.zeros_like(dva)
    scale = HS ** (-0.5)
    a = lax.broadcasted_iota(jnp.int32, (TILE, 2 * TILE), 0) + HALO
    b = lax.broadcasted_iota(jnp.int32, (TILE, 2 * TILE), 1)
    apart = a // CH - b // CH
    band = (apart >= -1) & (apart <= 1)
    diagonal = a == b

    def tile(t, carry):
        k0 = pl.multiple_of(t * TILE, TILE)
        q0 = pl.multiple_of(t * TILE + HALO, HALO)
        allowed = band & (
            diagonal | (qseg_ref[pl.ds(k0, TILE), :] == kcode_ref[t])
        )
        for h in range(cols // HS):
            sl = slice(h * HS, (h + 1) * HS)
            q = qe[pl.ds(q0, TILE), sl]
            g = ge[pl.ds(q0, TILE), sl]
            k = ke[pl.ds(k0, 2 * TILE), sl]
            v = ve[pl.ds(k0, 2 * TILE), sl]
            scores = jnp.where(allowed, mm(q, k, 1, 1) * scale, -1e30)
            weights = jnp.exp(scores - jnp.max(scores, axis=-1, keepdims=True))
            p = weights * (1.0 / jnp.sum(weights, axis=-1, keepdims=True))
            pb = p.astype(BF)
            dp = mm(g, v, 1, 1)
            delta = jnp.sum(p * dp, axis=-1, keepdims=True)
            ds = (p * (dp - delta) * scale).astype(BF)
            oe[pl.ds(q0, TILE), sl] = mm(pb, v, 1, 0).astype(BF)
            dqe[pl.ds(q0, TILE), sl] = mm(ds, k, 1, 0).astype(BF)
            dka[pl.ds(k0, 2 * TILE), sl] += mm(ds, q, 0, 0)
            dva[pl.ds(k0, 2 * TILE), sl] += mm(pb, g, 0, 0)
        return carry

    lax.fori_loop(0, rows // TILE + 1, tile, 0)
    o_ref[...] = oe[TILE:edge]
    dq_ref[...] = dqe[TILE:edge]
    dk_ref[...] = dka[TILE:edge].astype(BF)
    dv_ref[...] = dva[TILE:edge].astype(BF)


def attend(qseg, kcode, main, halo):
    rows, cols = main[0].shape
    ext = rows + 2 * TILE
    vmem = pl.BlockSpec(memory_space=pltpu.VMEM)
    return pl.pallas_call(
        attend_kernel,
        name="attend",
        in_specs=[vmem] * 10,
        out_specs=[vmem] * 4,
        out_shape=[jax.ShapeDtypeStruct((rows, cols), BF)] * 4,
        scratch_shapes=[pltpu.VMEM((ext, cols), BF)] * 6 + [pltpu.VMEM((ext, cols), F32)] * 2,
        compiler_params=pltpu.CompilerParams(vmem_limit_bytes=VMEM_LIMIT),
        cost_estimate=pl.CostEstimate(
            flops=24 * rows * TILE * cols, bytes_accessed=16 * rows * cols,
            transcendentals=rows * cols,
        ),
    )(qseg, kcode, *main, *halo)


def terms_kernel(normed_ref, masked_ref, o_ref, dq_ref, dk_ref, dv_ref, out_ref):
    cols = o_ref.shape[1]
    normed = normed_ref[...].T
    for piece, ref in enumerate((dq_ref, dk_ref, dv_ref)):
        out_ref[:, piece * cols : (piece + 1) * cols] = mm(normed, ref[...], 1, 0).astype(BF)
    out_ref[:, 3 * cols :] = mm(masked_ref[...].T, o_ref[...], 1, 0).astype(BF)


def weight_terms(normed, masked, o, dq, dk, dv):
    rows, depth = normed.shape
    cols = o.shape[1]
    step = 512
    part = pl.BlockSpec((rows, step), lambda i: (0, i))
    full = pl.BlockSpec((rows, cols), lambda i: (0, 0))
    return pl.pallas_call(
        terms_kernel,
        name="weight_terms",
        grid=(depth // step,),
        in_specs=[part, part, full, full, full, full],
        out_specs=pl.BlockSpec((step, 4 * cols), lambda i: (i, 0)),
        out_shape=jax.ShapeDtypeStruct((depth, 4 * cols), BF),
        compiler_params=pltpu.CompilerParams(vmem_limit_bytes=VMEM_LIMIT),
        cost_estimate=pl.CostEstimate(
            flops=8 * rows * depth * cols, bytes_accessed=8 * rows * depth, transcendentals=0
        ),
    )(normed, masked, o, dq, dk, dv)


def back_kernel(x_ref, gain_ref, w_ref, dq_ref, dk_ref, dv_ref, dy_ref, sums_ref):
    xhat, _ = norm_parts(x_ref[...])
    total = mm(dq_ref[...], w_ref[0], 1, 1)
    total += mm(dk_ref[...], w_ref[1], 1, 1)
    total += mm(dv_ref[...], w_ref[2], 1, 1)
    shares, _, width = dy_ref.shape
    for i in range(shares):
        dy_ref[i] = total[:, i * width : (i + 1) * width].astype(BF)
    scaled = total * gain_ref[...]
    first = jnp.sum(scaled, axis=-1, keepdims=True)
    second = jnp.sum(scaled * xhat, axis=-1, keepdims=True)
    lane = lax.broadcasted_iota(jnp.int32, sums_ref.shape, 1)
    sums_ref[...] = jnp.where(lane == 0, first, second)


def back(frames, gain, w, dq, dk, dv, shares):
    rows, depth = frames.shape
    cols = dq.shape[1]
    step = min(rows, 256)
    row = lambda width: pl.BlockSpec((step, width), lambda i: (i, 0))
    return pl.pallas_call(
        back_kernel,
        name="back",
        grid=(rows // step,),
        in_specs=[
            row(depth),
            pl.BlockSpec((1, depth), lambda i: (0, 0)),
            pl.BlockSpec(w.shape, lambda i: (0, 0, 0)),
            row(cols),
            row(cols),
            row(cols),
        ],
        out_specs=[
            pl.BlockSpec((shares, step, depth // shares), lambda i: (0, i, 0)),
            row(2),
        ],
        out_shape=[
            jax.ShapeDtypeStruct((shares, rows, depth // shares), BF),
            jax.ShapeDtypeStruct((rows, 2), F32),
        ],
        compiler_params=pltpu.CompilerParams(vmem_limit_bytes=VMEM_LIMIT),
        cost_estimate=pl.CostEstimate(
            flops=6 * rows * depth * cols, bytes_accessed=6 * rows * depth, transcendentals=0
        ),
    )(frames, gain, w, dq, dk, dv)


def final_kernel(depth, count, me_ref, x_ref, xs_ref, gain_ref, sums_ref, *refs):
    parts, out_ref = refs[:-1], refs[-1]
    values = x_ref[...].astype(F32)
    mean = jnp.mean(values, axis=-1, keepdims=True)
    center = values - mean
    inverse = lax.rsqrt(jnp.mean(center * center, axis=-1, keepdims=True) + EPSILON)
    xhat = (xs_ref[...].astype(F32) - mean) * inverse
    total = parts[0][0].astype(F32)
    for ref in parts[1:]:
        total += ref[0].astype(F32)
    scaled = total * gain_ref[...]
    first = sums_ref[:, 0:1] * (1.0 / depth)
    second = sums_ref[:, 1:2] * (1.0 / depth)
    out_ref[...] = (inverse * (scaled - first - xhat * second)).astype(BF)


def final(me, frames, gain, sums, own, received):
    rows, depth = frames.shape
    shares, _, width = own.shape
    step = min(rows, 256)
    return pl.pallas_call(
        functools.partial(final_kernel, depth, shares),
        name="final",
        grid_spec=pltpu.PrefetchScalarGridSpec(
            num_scalar_prefetch=1,
            grid=(rows // step,),
            in_specs=[
                pl.BlockSpec((step, depth), lambda i, me: (i, 0)),
                pl.BlockSpec((step, width), lambda i, me: (i, me[0])),
                pl.BlockSpec((1, width), lambda i, me: (0, me[0])),
                pl.BlockSpec((step, 2), lambda i, me: (i, 0)),
                pl.BlockSpec((1, step, width), lambda i, me: (me[0], i, 0)),
            ]
            + [pl.BlockSpec((1, step, width), lambda i, me: (0, i, 0))] * len(received),
            out_specs=pl.BlockSpec((step, width), lambda i, me: (i, 0)),
        ),
        out_shape=jax.ShapeDtypeStruct((rows, width), BF),
        compiler_params=pltpu.CompilerParams(vmem_limit_bytes=VMEM_LIMIT),
        cost_estimate=pl.CostEstimate(
            flops=8 * rows * depth, bytes_accessed=6 * rows * depth, transcendentals=0
        ),
    )(me, frames, frames, gain, sums, own, *received)


def neighbour_rows(frames, cot):
    count = lax.axis_size("tm")
    forward = [(i, i + 1) for i in range(count - 1)]
    backward = [(target, source) for source, target in forward]
    rows = frames.shape[0]
    top = jnp.stack([frames[rows - HALO :], cot[rows - HALO :]])
    bottom = jnp.stack([frames[:HALO], cot[:HALO]])
    low = lax.ppermute(top, "tm", forward)
    high = lax.ppermute(bottom, "tm", backward)
    return jnp.concatenate([low[0], high[0]]), jnp.concatenate([low[1], high[1]])


def on_device(frames, norm_gain, qkv_weight, out_weight, cotangent, pad_mask, utt_lengths):
    rows, depth = frames.shape
    cols = qkv_weight.shape[2]
    tm_count = lax.axis_size("tm")
    mp_count = lax.axis_size("mp")
    mp_at = lax.axis_index("mp")
    first_row = lax.axis_index("tm") * rows
    gain = norm_gain[None, :]

    ext = rows + 2 * TILE
    positions = first_row - TILE + jnp.arange(ext, dtype=jnp.int32)
    ends = jnp.cumsum(utt_lengths)
    segment = jnp.sum((ends[:, None] <= positions[None, :]).astype(jnp.int32), axis=0)
    live = lax.dynamic_slice(jnp.pad(pad_mask, TILE), (first_row,), (ext,))
    code = jnp.where(live == 1, segment, -1).reshape(-1, 1, TILE)
    kcode = jnp.concatenate([code[:-1], code[1:]], axis=2)
    qseg = segment[HALO : ext - HALO][:, None]
    live_main = live[TILE : TILE + rows][:, None]
    live_halo = jnp.concatenate(
        [live[TILE - HALO : TILE], live[TILE + rows : TILE + rows + HALO]]
    )[:, None]

    halo_frames, halo_cot = neighbour_rows(frames, cotangent)
    normed, masked, *main = project(
        frames, gain, qkv_weight, out_weight, cotangent, live_main
    )
    _, _, *halo = project(halo_frames, gain, qkv_weight, out_weight, halo_cot, live_halo)
    o, dq, dk, dv = attend(qseg, kcode, main, halo)

    terms = weight_terms(normed, masked, o, dq, dk, dv)
    summed = lax.psum_scatter(terms, "tm", scatter_dimension=0, tiled=True).astype(F32)
    share = depth // tm_count
    qkv_grad = summed[:, : 3 * cols].reshape(share, 3, cols).transpose(1, 0, 2)
    out_grad = summed[:, 3 * cols :].T

    dy, sums = back(frames, gain, qkv_weight, dq, dk, dv, mp_count)
    sums_flat = sums.T
    total = sums_flat
    received = []
    for shift in range(1, mp_count):
        pairs = [(i, (i + shift) % mp_count) for i in range(mp_count)]
        target = (mp_at + shift) % mp_count
        piece = lax.dynamic_slice_in_dim(dy, target, 1, 0)
        received.append(lax.ppermute(piece, "mp", pairs))
        total = total + lax.ppermute(sums_flat, "mp", pairs)
    me = jnp.reshape(mp_at, (1,)).astype(jnp.int32)
    frame_grad = final(me, frames, gain, total.T, dy, received)
    return (frame_grad, qkv_grad, out_grad)


def solution(mesh):
    placed = (
        P(("batch", "tm"), None),
        P(),
        P(None, None, "mp"),
        P("mp", None),
        P(("batch", "tm"), None),
        P("batch"),
        P("batch"),
    )
    return jax.shard_map(
        on_device,
        mesh=mesh,
        in_specs=placed,
        out_specs=(P(("batch", "tm"), "mp"), P("batch", "tm", "mp"), P(("batch", "mp"), "tm")),
        check_vma=False,
    )
```

```python
import functools

import jax
import jax.numpy as jnp
from jax import lax
from jax.experimental import pallas as pl
from jax.experimental.pallas import tpu as pltpu
from jax.sharding import PartitionSpec as P

HS = 128
CH = 32
HALO = 2 * CH
TILE = 128
EPSILON = 1e-05
VMEM_LIMIT = 60 * 1024 * 1024

BF = jnp.bfloat16
F32 = jnp.float32


def dims(contract_left, contract_right):
    return (((contract_left,), (contract_right,)), ((), ()))


def mm(left, right, contract_left, contract_right):
    return lax.dot_general(
        left, right, dims(contract_left, contract_right), preferred_element_type=F32
    )


def norm_parts(frames):
    values = frames.astype(F32)
    center = values - jnp.mean(values, axis=-1, keepdims=True)
    inverse = lax.rsqrt(jnp.mean(center * center, axis=-1, keepdims=True) + EPSILON)
    return center * inverse, inverse


def project_kernel(x_ref, gain_ref, w_ref, wo_ref, cot_ref, live_ref,
                   normed_ref, masked_ref, q_ref, k_ref, v_ref, g_ref):
    xhat, _ = norm_parts(x_ref[...])
    normed = (xhat * gain_ref[...]).astype(BF)
    normed_ref[...] = normed.T
    for piece, out in enumerate((q_ref, k_ref, v_ref)):
        out[...] = mm(normed, w_ref[piece], 1, 0).astype(BF)
    masked = jnp.where(live_ref[...] == 1, cot_ref[...].astype(F32), 0.0).astype(BF)
    masked_ref[...] = masked.T
    g_ref[...] = mm(masked, wo_ref[...], 1, 1).astype(BF)


def project(frames, gain, w, wo, cot, live):
    rows, depth = frames.shape
    cols = w.shape[2]
    step = min(rows, 256)
    row = lambda width: pl.BlockSpec((step, width), lambda i: (i, 0))
    return pl.pallas_call(
        project_kernel,
        name="project",
        grid=(rows // step,),
        in_specs=[
            row(depth),
            pl.BlockSpec((1, depth), lambda i: (0, 0)),
            pl.BlockSpec(w.shape, lambda i: (0, 0, 0)),
            pl.BlockSpec(wo.shape, lambda i: (0, 0)),
            row(depth),
            row(1),
        ],
        out_specs=[pl.BlockSpec((depth, step), lambda i: (0, i))] * 2 + [row(cols)] * 4,
        out_shape=[jax.ShapeDtypeStruct((depth, rows), BF)] * 2
        + [jax.ShapeDtypeStruct((rows, cols), BF)] * 4,
        compiler_params=pltpu.CompilerParams(vmem_limit_bytes=VMEM_LIMIT),
        cost_estimate=pl.CostEstimate(
            flops=8 * rows * depth * cols, bytes_accessed=8 * rows * depth, transcendentals=0
        ),
    )(frames, gain, w, wo, cot, live)


def backward_kernel(tm_count, mp_count, group_cols, block,
                    qseg_ref, kcode_ref, qm, km, vm, gm, qh, kh, vh, gh,
                    normed_t, masked_t, x_ref, gain_ref, w_ref,
                    frame_ref, qkv_ref, out_ref, *scratch):
    scratch = list(scratch)
    qe, ke, ve, ge, oe, dqe, dka, dva, dkb, dvb, stats, centre = scratch[:12]
    own, away, landed, sums_away, sums_landed = scratch[12:17]
    phases = tm_count.bit_length() - 1
    lists = scratch[17 : 17 + phases]
    arrivals = scratch[17 + phases : 17 + 2 * phases]
    (send_sem, recv_sem, share_send, share_recv, sums_send, sums_recv) = scratch[17 + 2 * phases :]
    rows, cols = qm.shape
    depth = x_ref.shape[1]
    share = depth // mp_count
    chunk = depth // tm_count
    groups = cols // group_cols
    edge = TILE + rows
    tm_at = lax.axis_index("tm")
    mp_at = lax.axis_index("mp")
    bits = [(tm_at // (1 << b)) % 2 for b in range(phases)]
    partners = [tm_at + (1 - 2 * bits[b]) * (1 << b) for b in range(phases)]
    mp_targets = [lax.rem(mp_at + shift, mp_count) for shift in range(1, mp_count)]

    barrier = pltpu.get_barrier_semaphore()
    for partner in partners:
        pl.semaphore_signal(barrier, inc=1, device_id={"tm": partner},
                            device_id_type=pl.DeviceIdType.MESH)
    for target in mp_targets:
        pl.semaphore_signal(barrier, inc=1, device_id={"mp": target},
                            device_id_type=pl.DeviceIdType.MESH)
    pl.semaphore_wait(barrier, phases + mp_count - 1)

    for ext, main, halo in ((qe, qm, qh), (ke, km, kh), (ve, vm, vh), (ge, gm, gh)):
        ext[0 : TILE - HALO] = jnp.zeros((TILE - HALO, cols), BF)
        ext[TILE - HALO : TILE] = halo[0:HALO]
        ext[TILE:edge] = main[...]
        ext[edge : edge + HALO] = halo[HALO : 2 * HALO]
        ext[edge + HALO : edge + TILE] = jnp.zeros((TILE - HALO, cols), BF)
    dka[...] = jnp.zeros_like(dka)
    dva[...] = jnp.zeros_like(dva)
    scale = HS ** (-0.5)
    a = lax.broadcasted_iota(jnp.int32, (TILE, 2 * TILE), 0) + HALO
    b = lax.broadcasted_iota(jnp.int32, (TILE, 2 * TILE), 1)
    apart = a // CH - b // CH
    band = (apart >= -1) & (apart <= 1)
    diagonal = a == b

    def attend(group, lo, hi):
        def tile(t, carry):
            k0 = pl.multiple_of(t * TILE, TILE)
            q0 = pl.multiple_of(t * TILE + HALO, HALO)
            allowed = band & (
                diagonal | (qseg_ref[pl.ds(k0, TILE), :] == kcode_ref[t])
            )
            for h in range(group * group_cols // HS, (group + 1) * group_cols // HS):
                sl = slice(h * HS, (h + 1) * HS)
                q = qe[pl.ds(q0, TILE), sl]
                g = ge[pl.ds(q0, TILE), sl]
                k = ke[pl.ds(k0, 2 * TILE), sl]
                v = ve[pl.ds(k0, 2 * TILE), sl]
                scores = jnp.where(allowed, mm(q, k, 1, 1) * scale, -1e30)
                weights = jnp.exp(scores - jnp.max(scores, axis=-1, keepdims=True))
                p = weights * (1.0 / jnp.sum(weights, axis=-1, keepdims=True))
                pb = p.astype(BF)
                dp = mm(g, v, 1, 1)
                delta = jnp.sum(p * dp, axis=-1, keepdims=True)
                ds = (p * (dp - delta) * scale).astype(BF)
                oe[pl.ds(q0, TILE), sl] = mm(pb, v, 1, 0).astype(BF)
                dqe[pl.ds(q0, TILE), sl] = mm(ds, k, 1, 0).astype(BF)
                dka[pl.ds(k0, 2 * TILE), sl] += mm(ds, q, 0, 0)
                dva[pl.ds(k0, 2 * TILE), sl] += mm(pb, g, 0, 0)
            return carry

        lax.fori_loop(lo, hi, tile, 0)

    def close(group):
        sl = slice(group * group_cols, (group + 1) * group_cols)
        dkb[:, sl] = dka[TILE:edge, sl].astype(BF)
        dvb[:, sl] = dva[TILE:edge, sl].astype(BF)

    def copy(unit, b):
        return pltpu.make_async_remote_copy(
            src_ref=lists[b].at[unit, :, 1 - bits[b]],
            dst_ref=arrivals[b].at[unit],
            send_sem=send_sem.at[unit, b],
            recv_sem=recv_sem.at[unit, b],
            device_id={"tm": partners[b]},
            device_id_type=pl.DeviceIdType.MESH,
        )

    copies = {}
    progress = {}
    step = 256

    def terms(unit):
        group, half = unit // 2, unit % 2
        sl = slice(group * group_cols, (group + 1) * group_cols)
        pairs = (
            ((normed_t, dqe[TILE:edge, sl]), (normed_t, dkb[:, sl]))
            if half == 0
            else ((normed_t, dvb[:, sl]), (masked_t, oe[TILE:edge, sl]))
        )
        for at in range(0, depth, step):
            for side, (left, right) in enumerate(pairs):
                part = mm(left[at : at + step], right, 1, 0).astype(BF)
                for r in range(0, step, chunk):
                    owner = (at + r) // chunk
                    lists[0][unit, owner // 2, owner % 2, :,
                             side * group_cols : (side + 1) * group_cols] = part[r : r + chunk]
        copies[unit, 0] = copy(unit, 0)
        copies[unit, 0].start()
        progress[unit] = 0

    def advance(unit):
        b = progress[unit]
        copies[unit, b].wait_recv()
        if b < phases - 1:
            for j in range(tm_count >> (b + 1)):
                kept = lists[b][unit, j, bits[b]].astype(F32) + arrivals[b][unit, j].astype(F32)
                lists[b + 1][unit, j // 2, j % 2] = kept.astype(BF)
            copies[unit, b + 1] = copy(unit, b + 1)
            copies[unit, b + 1].start()
        else:
            kept = lists[b][unit, 0, bits[b]].astype(F32) + arrivals[b][unit, 0].astype(F32)
            group, half = unit // 2, unit % 2
            sl = slice(group * group_cols, (group + 1) * group_cols)
            first, second = kept[:, :group_cols], kept[:, group_cols:]
            if half == 0:
                qkv_ref[0, :, sl] = first
                qkv_ref[1, :, sl] = second
            else:
                qkv_ref[2, :, sl] = first
                out_ref[sl, :] = second.T
        progress[unit] = b + 1

    def moments():
        for r in range(0, rows, block):
            values = x_ref[r : r + block].astype(F32)
            mean = jnp.mean(values, axis=-1, keepdims=True)
            center = values - mean
            inverse = lax.rsqrt(jnp.mean(center * center, axis=-1, keepdims=True) + EPSILON)
            centre[r : r + block, 0:1] = mean
            centre[r : r + block, 1:2] = inverse

    def incoming(target, r):
        lane = pl.multiple_of(target * share, 128)
        span = pl.ds(lane, share)
        total = mm(dqe[TILE + r : TILE + r + block], w_ref[0, span, :], 1, 1)
        total += mm(dkb[r : r + block], w_ref[1, span, :], 1, 1)
        total += mm(dvb[r : r + block], w_ref[2, span, :], 1, 1)
        xhat = (x_ref[r : r + block, span].astype(F32) - centre[r : r + block, 0:1]) * centre[
            r : r + block, 1:2
        ]
        scaled = total * gain_ref[:, span]
        first = jnp.sum(scaled, axis=-1, keepdims=True)
        second = jnp.sum(scaled * xhat, axis=-1, keepdims=True)
        return total, first, second

    shares = {}

    def away_shares():
        for s, target in enumerate(mp_targets):
            for i, r in enumerate(range(0, rows, block)):
                total, first, second = incoming(target, r)
                away[s, r : r + block] = total.astype(BF)
                shares[s, i] = pltpu.make_async_remote_copy(
                    src_ref=away.at[s, pl.ds(r, block)],
                    dst_ref=landed.at[s, pl.ds(r, block)],
                    send_sem=share_send.at[s, i],
                    recv_sem=share_recv.at[s, i],
                    device_id={"mp": target},
                    device_id_type=pl.DeviceIdType.MESH,
                )
                shares[s, i].start()
                if s == 0:
                    stats[r : r + block, 0:1] = first
                    stats[r : r + block, 1:2] = second
                else:
                    stats[r : r + block, 0:1] += first
                    stats[r : r + block, 1:2] += second

    def own_share():
        for r in range(0, rows, block):
            total, first, second = incoming(mp_at, r)
            own[r : r + block] = total
            if mp_count > 1:
                first += stats[r : r + block, 0:1]
                second += stats[r : r + block, 1:2]
            lane = lax.broadcasted_iota(jnp.int32, (block, 128), 1)
            both = jnp.where(lane == 0, first, second)
            sums_away[:, r : r + block] = both.T[0:8]
        for s, target in enumerate(mp_targets):
            shares[s, -1] = pltpu.make_async_remote_copy(
                src_ref=sums_away,
                dst_ref=sums_landed.at[s],
                send_sem=sums_send.at[s],
                recv_sem=sums_recv.at[s],
                device_id={"mp": target},
                device_id_type=pl.DeviceIdType.MESH,
            )
            shares[s, -1].start()

    def norm_rows():
        span = pl.ds(pl.multiple_of(mp_at * share, 128), share)
        for s in range(mp_count - 1):
            shares[s, -1].wait_recv()
        for i, r in enumerate(range(0, rows, block)):
            total = own[r : r + block]
            both = sums_away[:, r : r + block]
            for s in range(mp_count - 1):
                shares[s, i].wait_recv()
                total += landed[s, r : r + block].astype(F32)
                both += sums_landed[s, :, r : r + block]
            both = both.T * (1.0 / depth)
            inverse = centre[r : r + block, 1:2]
            xhat = (x_ref[r : r + block, span].astype(F32) - centre[r : r + block, 0:1]) * inverse
            scaled = total * gain_ref[:, span]
            frame_ref[r : r + block] = (
                inverse * (scaled - both[:, 0:1] - xhat * both[:, 1:2])
            ).astype(BF)

    tiles = rows // TILE + 1
    for group in range(groups - 1):
        if group == 0:
            attend(group, 0, tiles)
        close(group)
        terms(2 * group)
        terms(2 * group + 1)
        advance(2 * group)
        third = tiles // 3
        attend(group + 1, 0, third)
        advance(2 * group + 1)
        attend(group + 1, third, 2 * third)
        if phases > 1:
            advance(2 * group)
        attend(group + 1, 2 * third, tiles)
        if phases > 1:
            advance(2 * group + 1)
    if groups == 1:
        attend(0, 0, tiles)
    close(groups - 1)
    moments()
    away_shares()
    terms(2 * groups - 2)
    terms(2 * groups - 1)
    advance(2 * groups - 2)
    own_share()
    for b in range(phases):
        for unit in range(2 * groups):
            if progress[unit] == b:
                advance(unit)
    norm_rows()
    for unit in range(2 * groups):
        for b in range(phases):
            copies[unit, b].wait_send()
    for item in shares.values():
        item.wait_send()


def backward(qseg, kcode, main, halo, normed_t, masked_t, frames, gain, w, tm_count, mp_count):
    rows, cols = main[0].shape
    depth = frames.shape[1]
    ext = rows + 2 * TILE
    share = depth // mp_count
    chunk = depth // tm_count
    group_cols = min(cols, 2 * HS)
    units = 2 * (cols // group_cols)
    width = 2 * group_cols
    block = min(rows, 256)
    blocks = rows // block
    peers = max(mp_count - 1, 1)
    phases = tm_count.bit_length() - 1
    vmem = pl.BlockSpec(memory_space=pltpu.VMEM)
    dma = pltpu.SemaphoreType.DMA
    return pl.pallas_call(
        functools.partial(backward_kernel, tm_count, mp_count, group_cols, block),
        name="backward",
        in_specs=[vmem] * 15,
        out_specs=[vmem] * 3,
        out_shape=[
            jax.ShapeDtypeStruct((rows, share), BF),
            jax.ShapeDtypeStruct((3, chunk, cols), F32),
            jax.ShapeDtypeStruct((cols, chunk), F32),
        ],
        scratch_shapes=[pltpu.VMEM((ext, cols), BF)] * 6
        + [pltpu.VMEM((ext, cols), F32)] * 2
        + [pltpu.VMEM((rows, cols), BF)] * 2
        + [pltpu.VMEM((rows, 2), F32)] * 2
        + [
            pltpu.VMEM((rows, share), F32),
            pltpu.VMEM((peers, rows, share), BF),
            pltpu.VMEM((peers, rows, share), BF),
            pltpu.VMEM((8, rows), F32),
            pltpu.VMEM((peers, 8, rows), F32),
        ]
        + [
            pltpu.VMEM((units, tm_count >> (b + 1), 2, chunk, width), BF) for b in range(phases)
        ]
        + [pltpu.VMEM((units, tm_count >> (b + 1), chunk, width), BF) for b in range(phases)]
        + [
            dma((units, phases)),
            dma((units, phases)),
            dma((peers, blocks)),
            dma((peers, blocks)),
            dma((peers,)),
            dma((peers,)),
        ],
        compiler_params=pltpu.CompilerParams(
            vmem_limit_bytes=VMEM_LIMIT, collective_id=0, has_side_effects=True
        ),
        cost_estimate=pl.CostEstimate(
            flops=24 * rows * depth * cols, bytes_accessed=30 * rows * depth,
            transcendentals=rows * cols,
        ),
    )(qseg, kcode, *main, *halo, normed_t, masked_t, frames, gain, w)


def neighbour_rows(frames, cot):
    count = lax.axis_size("tm")
    forward = [(i, i + 1) for i in range(count - 1)]
    backward = [(target, source) for source, target in forward]
    rows = frames.shape[0]
    top = jnp.stack([frames[rows - HALO :], cot[rows - HALO :]])
    bottom = jnp.stack([frames[:HALO], cot[:HALO]])
    low = lax.ppermute(top, "tm", forward)
    high = lax.ppermute(bottom, "tm", backward)
    return jnp.concatenate([low[0], high[0]]), jnp.concatenate([low[1], high[1]])


def on_device(frames, norm_gain, qkv_weight, out_weight, cotangent, pad_mask, utt_lengths):
    rows = frames.shape[0]
    tm_count = lax.axis_size("tm")
    mp_count = lax.axis_size("mp")
    first_row = lax.axis_index("tm") * rows
    gain = norm_gain[None, :]

    ext = rows + 2 * TILE
    positions = first_row - TILE + jnp.arange(ext, dtype=jnp.int32)
    ends = jnp.cumsum(utt_lengths)
    segment = jnp.sum((ends[:, None] <= positions[None, :]).astype(jnp.int32), axis=0)
    live = lax.dynamic_slice(jnp.pad(pad_mask, TILE), (first_row,), (ext,))
    code = jnp.where(live == 1, segment, -1).reshape(-1, 1, TILE)
    kcode = jnp.concatenate([code[:-1], code[1:]], axis=2)
    qseg = segment[HALO : ext - HALO][:, None]
    live_main = live[TILE : TILE + rows][:, None]
    live_halo = jnp.concatenate(
        [live[TILE - HALO : TILE], live[TILE + rows : TILE + rows + HALO]]
    )[:, None]

    halo_frames, halo_cot = neighbour_rows(frames, cotangent)
    normed_t, masked_t, *main = project(
        frames, gain, qkv_weight, out_weight, cotangent, live_main
    )
    _, _, *halo = project(halo_frames, gain, qkv_weight, out_weight, halo_cot, live_halo)
    return tuple(
        backward(
            qseg, kcode, main, halo, normed_t, masked_t, frames, gain, qkv_weight,
            tm_count, mp_count,
        )
    )


def solution(mesh):
    placed = (
        P(("batch", "tm"), None),
        P(),
        P(None, None, "mp"),
        P("mp", None),
        P(("batch", "tm"), None),
        P("batch"),
        P("batch"),
    )
    return jax.shard_map(
        on_device,
        mesh=mesh,
        in_specs=placed,
        out_specs=(P(("batch", "tm"), "mp"), P("batch", "tm", "mp"), P(("batch", "mp"), "tm")),
        check_vma=False,
    )
```

```python
import functools

import jax
import jax.numpy as jnp
from jax import lax
from jax.experimental import pallas as pl
from jax.experimental.pallas import tpu as pltpu
from jax.sharding import PartitionSpec as P

HS = 128
CH = 32
HALO = 2 * CH
TILE = 128
EPSILON = 1e-05
VMEM_LIMIT = 60 * 1024 * 1024

BF = jnp.bfloat16
F32 = jnp.float32


def dims(contract_left, contract_right):
    return (((contract_left,), (contract_right,)), ((), ()))


def mm(left, right, contract_left, contract_right):
    return lax.dot_general(
        left, right, dims(contract_left, contract_right), preferred_element_type=F32
    )


def backward_kernel(tm_count, mp_count, group_cols, block,
                    query_ref, kcode_ref, x_ref, cot_ref, gain_ref, w_ref, wo_ref,
                    frame_ref, qkv_ref, out_ref, *scratch):
    scratch = list(scratch)
    halo_x, halo_cot, normed_t, masked_t, halo_send, halo_recv = scratch[:6]
    scratch = scratch[6:]
    qe, ke, ve, ge, oe, dqe, dka, dva, dkb, dvb, stats, centre = scratch[:12]
    own, away, landed, sums_away, sums_landed = scratch[12:17]
    phases = tm_count.bit_length() - 1
    lists = scratch[17 : 17 + phases]
    arrivals = scratch[17 + phases : 17 + 2 * phases]
    (send_sem, recv_sem, share_send, share_recv, sums_send, sums_recv) = scratch[17 + 2 * phases :]
    rows, depth = x_ref.shape
    cols = w_ref.shape[2]
    share = depth // mp_count
    chunk = depth // tm_count
    groups = cols // group_cols
    edge = TILE + rows
    tm_at = lax.axis_index("tm")
    mp_at = lax.axis_index("mp")
    bits = [(tm_at // (1 << b)) % 2 for b in range(phases)]
    partners = [tm_at + (1 - 2 * bits[b]) * (1 << b) for b in range(phases)]
    mp_targets = [lax.rem(mp_at + shift, mp_count) for shift in range(1, mp_count)]

    after = lax.rem(tm_at + 1, tm_count)
    before = lax.rem(tm_at + tm_count - 1, tm_count)

    barrier = pltpu.get_barrier_semaphore()
    for partner in partners + [after, before]:
        pl.semaphore_signal(barrier, inc=1, device_id={"tm": partner},
                            device_id_type=pl.DeviceIdType.MESH)
    for target in mp_targets:
        pl.semaphore_signal(barrier, inc=1, device_id={"mp": target},
                            device_id_type=pl.DeviceIdType.MESH)
    pl.semaphore_wait(barrier, phases + mp_count + 1)

    halos = []
    for source, target in ((x_ref, halo_x), (cot_ref, halo_cot)):
        for start, slot, device in ((rows - HALO, 0, after), (0, 1, before)):
            halos.append(
                pltpu.make_async_remote_copy(
                    src_ref=source.at[pl.ds(start, HALO)],
                    dst_ref=target.at[pl.ds(slot * HALO, HALO)],
                    send_sem=halo_send.at[len(halos)],
                    recv_sem=halo_recv.at[len(halos)],
                    device_id={"tm": device},
                    device_id_type=pl.DeviceIdType.MESH,
                )
            )
    for item in halos:
        item.start()

    for ext in (qe, ke, ve, ge):
        ext[0 : TILE - HALO] = jnp.zeros((TILE - HALO, cols), BF)
        ext[edge + HALO : edge + TILE] = jnp.zeros((TILE - HALO, cols), BF)

    def project(values, cot, live):
        mean = jnp.mean(values, axis=-1, keepdims=True)
        center = values - mean
        inverse = lax.rsqrt(jnp.mean(center * center, axis=-1, keepdims=True) + EPSILON)
        normed = (center * inverse * gain_ref[...]).astype(BF)
        masked = jnp.where(live == 1, cot.astype(F32), 0.0).astype(BF)
        outs = [mm(normed, w_ref[piece], 1, 0).astype(BF) for piece in range(3)]
        outs.append(mm(masked, wo_ref[...], 1, 1).astype(BF))
        return mean, inverse, normed, masked, outs

    def project_rows(i, carry):
        r = pl.multiple_of(i * block, block)
        mean, inverse, normed, masked, outs = project(
            x_ref[pl.ds(r, block), :].astype(F32),
            cot_ref[pl.ds(r, block), :],
            query_ref[pl.ds(r + HALO, block), 1:2],
        )
        centre[pl.ds(r, block), 0:1] = mean
        centre[pl.ds(r, block), 1:2] = inverse
        normed_t[:, pl.ds(r, block)] = normed.T
        masked_t[:, pl.ds(r, block)] = masked.T
        for ext, out in zip((qe, ke, ve, ge), outs):
            ext[pl.ds(r + TILE, block), :] = out
        return carry

    lax.fori_loop(0, rows // block, project_rows, 0)
    for item in halos:
        item.wait_recv()
    at_row = lax.broadcasted_iota(jnp.int32, (2 * HALO, 1), 0)
    inside = jnp.where(
        at_row < HALO,
        jnp.where(tm_at > 0, 1, 0),
        jnp.where(tm_at < tm_count - 1, 1, 0),
    )
    live = jnp.concatenate(
        [query_ref[0:HALO, 1:2], query_ref[HALO + rows : 2 * HALO + rows, 1:2]]
    )
    outs = project(
        jnp.where(inside == 1, halo_x[...].astype(F32), 0.0), halo_cot[...], live
    )[-1]
    for ext, out in zip((qe, ke, ve, ge), outs):
        ext[TILE - HALO : TILE] = out[:HALO]
        ext[edge : edge + HALO] = out[HALO:]

    dka[...] = jnp.zeros_like(dka)
    dva[...] = jnp.zeros_like(dva)
    scale = HS ** (-0.5)
    a = lax.broadcasted_iota(jnp.int32, (TILE, 2 * TILE), 0) + HALO
    b = lax.broadcasted_iota(jnp.int32, (TILE, 2 * TILE), 1)
    apart = a // CH - b // CH
    band = (apart >= -1) & (apart <= 1)
    diagonal = a == b

    def attend(group, lo, hi):
        def tile(t, carry):
            k0 = pl.multiple_of(t * TILE, TILE)
            q0 = pl.multiple_of(t * TILE + HALO, HALO)
            allowed = band & (
                diagonal | (query_ref[pl.ds(k0, TILE), 0:1] == kcode_ref[t])
            )
            for h in range(group * group_cols // HS, (group + 1) * group_cols // HS):
                sl = slice(h * HS, (h + 1) * HS)
                q = qe[pl.ds(q0, TILE), sl]
                g = ge[pl.ds(q0, TILE), sl]
                k = ke[pl.ds(k0, 2 * TILE), sl]
                v = ve[pl.ds(k0, 2 * TILE), sl]
                scores = jnp.where(allowed, mm(q, k, 1, 1) * scale, -1e30)
                weights = jnp.exp(scores - jnp.max(scores, axis=-1, keepdims=True))
                p = weights * (1.0 / jnp.sum(weights, axis=-1, keepdims=True))
                pb = p.astype(BF)
                dp = mm(g, v, 1, 1)
                delta = jnp.sum(p * dp, axis=-1, keepdims=True)
                ds = (p * (dp - delta) * scale).astype(BF)
                oe[pl.ds(q0, TILE), sl] = mm(pb, v, 1, 0).astype(BF)
                dqe[pl.ds(q0, TILE), sl] = mm(ds, k, 1, 0).astype(BF)
                dka[pl.ds(k0, 2 * TILE), sl] += mm(ds, q, 0, 0)
                dva[pl.ds(k0, 2 * TILE), sl] += mm(pb, g, 0, 0)
            return carry

        lax.fori_loop(lo, hi, tile, 0)

    def close(group):
        sl = slice(group * group_cols, (group + 1) * group_cols)
        dkb[:, sl] = dka[TILE:edge, sl].astype(BF)
        dvb[:, sl] = dva[TILE:edge, sl].astype(BF)

    def copy(unit, b):
        return pltpu.make_async_remote_copy(
            src_ref=lists[b].at[unit, :, 1 - bits[b]],
            dst_ref=arrivals[b].at[unit],
            send_sem=send_sem.at[unit, b],
            recv_sem=recv_sem.at[unit, b],
            device_id={"tm": partners[b]},
            device_id_type=pl.DeviceIdType.MESH,
        )

    copies = {}
    progress = {}
    step = 256

    def terms(unit):
        group, half = unit // 2, unit % 2
        sl = slice(group * group_cols, (group + 1) * group_cols)
        pairs = (
            ((normed_t, dqe[TILE:edge, sl]), (normed_t, dkb[:, sl]))
            if half == 0
            else ((normed_t, dvb[:, sl]), (masked_t, oe[TILE:edge, sl]))
        )
        for at in range(0, depth, step):
            for side, (left, right) in enumerate(pairs):
                part = mm(left[at : at + step], right, 1, 0).astype(BF)
                for r in range(0, step, chunk):
                    owner = (at + r) // chunk
                    lists[0][unit, owner // 2, owner % 2, :,
                             side * group_cols : (side + 1) * group_cols] = part[r : r + chunk]
        copies[unit, 0] = copy(unit, 0)
        copies[unit, 0].start()
        progress[unit] = 0

    def advance(unit):
        b = progress[unit]
        copies[unit, b].wait_recv()
        if b < phases - 1:
            for j in range(tm_count >> (b + 1)):
                kept = lists[b][unit, j, bits[b]].astype(F32) + arrivals[b][unit, j].astype(F32)
                lists[b + 1][unit, j // 2, j % 2] = kept.astype(BF)
            copies[unit, b + 1] = copy(unit, b + 1)
            copies[unit, b + 1].start()
        else:
            kept = lists[b][unit, 0, bits[b]].astype(F32) + arrivals[b][unit, 0].astype(F32)
            group, half = unit // 2, unit % 2
            sl = slice(group * group_cols, (group + 1) * group_cols)
            first, second = kept[:, :group_cols], kept[:, group_cols:]
            if half == 0:
                qkv_ref[0, :, sl] = first
                qkv_ref[1, :, sl] = second
            else:
                qkv_ref[2, :, sl] = first
                out_ref[sl, :] = second.T
        progress[unit] = b + 1

    def incoming(target, r):
        lane = pl.multiple_of(target * share, 128)
        span = pl.ds(lane, share)
        total = mm(dqe[TILE + r : TILE + r + block], w_ref[0, span, :], 1, 1)
        total += mm(dkb[r : r + block], w_ref[1, span, :], 1, 1)
        total += mm(dvb[r : r + block], w_ref[2, span, :], 1, 1)
        xhat = (x_ref[r : r + block, span].astype(F32) - centre[r : r + block, 0:1]) * centre[
            r : r + block, 1:2
        ]
        scaled = total * gain_ref[:, span]
        first = jnp.sum(scaled, axis=-1, keepdims=True)
        second = jnp.sum(scaled * xhat, axis=-1, keepdims=True)
        return total, first, second

    shares = {}

    def away_shares():
        for s, target in enumerate(mp_targets):
            for i, r in enumerate(range(0, rows, block)):
                total, first, second = incoming(target, r)
                away[s, r : r + block] = total.astype(BF)
                shares[s, i] = pltpu.make_async_remote_copy(
                    src_ref=away.at[s, pl.ds(r, block)],
                    dst_ref=landed.at[s, pl.ds(r, block)],
                    send_sem=share_send.at[s, i],
                    recv_sem=share_recv.at[s, i],
                    device_id={"mp": target},
                    device_id_type=pl.DeviceIdType.MESH,
                )
                shares[s, i].start()
                if s == 0:
                    stats[r : r + block, 0:1] = first
                    stats[r : r + block, 1:2] = second
                else:
                    stats[r : r + block, 0:1] += first
                    stats[r : r + block, 1:2] += second

    def own_share():
        for r in range(0, rows, block):
            total, first, second = incoming(mp_at, r)
            own[r : r + block] = total
            if mp_count > 1:
                first += stats[r : r + block, 0:1]
                second += stats[r : r + block, 1:2]
            lane = lax.broadcasted_iota(jnp.int32, (block, 128), 1)
            both = jnp.where(lane == 0, first, second)
            sums_away[:, r : r + block] = both.T[0:8]
        for s, target in enumerate(mp_targets):
            shares[s, -1] = pltpu.make_async_remote_copy(
                src_ref=sums_away,
                dst_ref=sums_landed.at[s],
                send_sem=sums_send.at[s],
                recv_sem=sums_recv.at[s],
                device_id={"mp": target},
                device_id_type=pl.DeviceIdType.MESH,
            )
            shares[s, -1].start()

    def norm_rows():
        span = pl.ds(pl.multiple_of(mp_at * share, 128), share)
        for s in range(mp_count - 1):
            shares[s, -1].wait_recv()
        for i, r in enumerate(range(0, rows, block)):
            total = own[r : r + block]
            both = sums_away[:, r : r + block]
            for s in range(mp_count - 1):
                shares[s, i].wait_recv()
                total += landed[s, r : r + block].astype(F32)
                both += sums_landed[s, :, r : r + block]
            both = both.T * (1.0 / depth)
            inverse = centre[r : r + block, 1:2]
            xhat = (x_ref[r : r + block, span].astype(F32) - centre[r : r + block, 0:1]) * inverse
            scaled = total * gain_ref[:, span]
            frame_ref[r : r + block] = (
                inverse * (scaled - both[:, 0:1] - xhat * both[:, 1:2])
            ).astype(BF)

    tiles = rows // TILE + 1
    for group in range(groups - 1):
        if group == 0:
            attend(group, 0, tiles)
        close(group)
        terms(2 * group)
        terms(2 * group + 1)
        advance(2 * group)
        third = tiles // 3
        attend(group + 1, 0, third)
        advance(2 * group + 1)
        attend(group + 1, third, 2 * third)
        if phases > 1:
            advance(2 * group)
        attend(group + 1, 2 * third, tiles)
        if phases > 1:
            advance(2 * group + 1)
    if groups == 1:
        attend(0, 0, tiles)
    close(groups - 1)
    away_shares()
    terms(2 * groups - 2)
    terms(2 * groups - 1)
    advance(2 * groups - 2)
    own_share()
    for b in range(phases):
        for unit in range(2 * groups):
            if progress[unit] == b:
                advance(unit)
    norm_rows()
    for item in halos:
        item.wait_send()
    for unit in range(2 * groups):
        for b in range(phases):
            copies[unit, b].wait_send()
    for item in shares.values():
        item.wait_send()


def backward(query, kcode, frames, cot, gain, w, wo, tm_count, mp_count):
    rows, depth = frames.shape
    cols = w.shape[2]
    ext = rows + 2 * TILE
    share = depth // mp_count
    chunk = depth // tm_count
    group_cols = min(cols, 2 * HS)
    units = 2 * (cols // group_cols)
    width = 2 * group_cols
    block = min(rows, 256)
    blocks = rows // block
    peers = max(mp_count - 1, 1)
    phases = tm_count.bit_length() - 1
    vmem = pl.BlockSpec(memory_space=pltpu.VMEM)
    dma = pltpu.SemaphoreType.DMA
    return pl.pallas_call(
        functools.partial(backward_kernel, tm_count, mp_count, group_cols, block),
        name="backward",
        in_specs=[vmem] * 7,
        out_specs=[vmem] * 3,
        out_shape=[
            jax.ShapeDtypeStruct((rows, share), BF),
            jax.ShapeDtypeStruct((3, chunk, cols), F32),
            jax.ShapeDtypeStruct((cols, chunk), F32),
        ],
        scratch_shapes=[pltpu.VMEM((2 * HALO, depth), BF)] * 2
        + [pltpu.VMEM((depth, rows), BF)] * 2
        + [dma((4,))] * 2
        + [pltpu.VMEM((ext, cols), BF)] * 6
        + [pltpu.VMEM((ext, cols), F32)] * 2
        + [pltpu.VMEM((rows, cols), BF)] * 2
        + [pltpu.VMEM((rows, 2), F32)] * 2
        + [
            pltpu.VMEM((rows, share), F32),
            pltpu.VMEM((peers, rows, share), BF),
            pltpu.VMEM((peers, rows, share), BF),
            pltpu.VMEM((8, rows), F32),
            pltpu.VMEM((peers, 8, rows), F32),
        ]
        + [
            pltpu.VMEM((units, tm_count >> (b + 1), 2, chunk, width), BF) for b in range(phases)
        ]
        + [pltpu.VMEM((units, tm_count >> (b + 1), chunk, width), BF) for b in range(phases)]
        + [
            dma((units, phases)),
            dma((units, phases)),
            dma((peers, blocks)),
            dma((peers, blocks)),
            dma((peers,)),
            dma((peers,)),
        ],
        compiler_params=pltpu.CompilerParams(
            vmem_limit_bytes=VMEM_LIMIT, collective_id=0, has_side_effects=True
        ),
        cost_estimate=pl.CostEstimate(
            flops=24 * rows * depth * cols, bytes_accessed=30 * rows * depth,
            transcendentals=rows * cols,
        ),
    )(query, kcode, frames, cot, gain, w, wo)


def on_device(frames, norm_gain, qkv_weight, out_weight, cotangent, pad_mask, utt_lengths):
    rows = frames.shape[0]
    tm_count = lax.axis_size("tm")
    mp_count = lax.axis_size("mp")
    first_row = lax.axis_index("tm") * rows
    gain = norm_gain[None, :]

    ext = rows + 2 * TILE
    positions = first_row - TILE + jnp.arange(ext, dtype=jnp.int32)
    ends = jnp.cumsum(utt_lengths)
    segment = jnp.sum((ends[:, None] <= positions[None, :]).astype(jnp.int32), axis=0)
    live = lax.dynamic_slice(jnp.pad(pad_mask, TILE), (first_row,), (ext,))
    code = jnp.where(live == 1, segment, -1).reshape(-1, 1, TILE)
    kcode = jnp.concatenate([code[:-1], code[1:]], axis=2)
    query = jnp.stack([segment, live], axis=1)[HALO : ext - HALO]
    return tuple(
        backward(
            query, kcode, frames, cotangent, gain, qkv_weight, out_weight, tm_count, mp_count
        )
    )


def solution(mesh):
    placed = (
        P(("batch", "tm"), None),
        P(),
        P(None, None, "mp"),
        P("mp", None),
        P(("batch", "tm"), None),
        P("batch"),
        P("batch"),
    )
    return jax.shard_map(
        on_device,
        mesh=mesh,
        in_specs=placed,
        out_specs=(P(("batch", "tm"), "mp"), P("batch", "tm", "mp"), P(("batch", "mp"), "tm")),
        check_vma=False,
    )
```

```python
import functools

import jax
import jax.numpy as jnp
from jax import lax
from jax.experimental import pallas as pl
from jax.experimental.pallas import tpu as pltpu
from jax.sharding import PartitionSpec as P

HS = 128
CH = 32
HALO = 2 * CH
TILE = 128
EPSILON = 1e-05
VMEM_LIMIT = 60 * 1024 * 1024

BF = jnp.bfloat16
F32 = jnp.float32


def dims(contract_left, contract_right):
    return (((contract_left,), (contract_right,)), ((), ()))


def mm(left, right, contract_left, contract_right):
    return lax.dot_general(
        left, right, dims(contract_left, contract_right), preferred_element_type=F32
    )


def backward_kernel(tm_count, mp_count, group_cols, block,
                    query_ref, kcode_ref, x_ref, cot_ref, gain_ref, w_ref, wo_ref,
                    frame_ref, qkv_ref, out_ref, *scratch):
    scratch = list(scratch)
    halo_x, halo_cot, normed_t, masked_t, halo_send, halo_recv = scratch[:6]
    scratch = scratch[6:]
    qe, ke, ve, ge, oe, dqe, dka, dva, dkb, dvb, stats, centre = scratch[:12]
    own, away, landed, sums_away, sums_landed = scratch[12:17]
    phases = tm_count.bit_length() - 1
    lists = scratch[17 : 17 + phases]
    arrivals = scratch[17 + phases : 17 + 2 * phases]
    (send_sem, recv_sem, share_send, share_recv, sums_send, sums_recv) = scratch[17 + 2 * phases :]
    rows, depth = x_ref.shape
    cols = w_ref.shape[2]
    share = depth // mp_count
    chunk = depth // tm_count
    groups = cols // group_cols
    edge = TILE + rows
    tm_at = lax.axis_index("tm")
    mp_at = lax.axis_index("mp")
    bits = [(tm_at // (1 << b)) % 2 for b in range(phases)]
    partners = [tm_at + (1 - 2 * bits[b]) * (1 << b) for b in range(phases)]
    mp_targets = [lax.rem(mp_at + shift, mp_count) for shift in range(1, mp_count)]

    after = lax.rem(tm_at + 1, tm_count)
    before = lax.rem(tm_at + tm_count - 1, tm_count)

    barrier = pltpu.get_barrier_semaphore()
    for partner in partners + [after, before]:
        pl.semaphore_signal(barrier, inc=1, device_id={"tm": partner},
                            device_id_type=pl.DeviceIdType.MESH)
    for target in mp_targets:
        pl.semaphore_signal(barrier, inc=1, device_id={"mp": target},
                            device_id_type=pl.DeviceIdType.MESH)
    pl.semaphore_wait(barrier, phases + mp_count + 1)

    halos = []
    for source, target in ((x_ref, halo_x), (cot_ref, halo_cot)):
        for start, slot, device in ((rows - HALO, 0, after), (0, 1, before)):
            halos.append(
                pltpu.make_async_remote_copy(
                    src_ref=source.at[pl.ds(start, HALO)],
                    dst_ref=target.at[pl.ds(slot * HALO, HALO)],
                    send_sem=halo_send.at[len(halos)],
                    recv_sem=halo_recv.at[len(halos)],
                    device_id={"tm": device},
                    device_id_type=pl.DeviceIdType.MESH,
                )
            )
    for item in halos:
        item.start()

    for ext in (qe, ke, ve, ge):
        ext[0 : TILE - HALO] = jnp.zeros((TILE - HALO, cols), BF)
        ext[edge + HALO : edge + TILE] = jnp.zeros((TILE - HALO, cols), BF)

    def project(values, cot, live):
        mean = jnp.mean(values, axis=-1, keepdims=True)
        center = values - mean
        inverse = lax.rsqrt(jnp.mean(center * center, axis=-1, keepdims=True) + EPSILON)
        normed = (center * inverse * gain_ref[...]).astype(BF)
        masked = jnp.where(live == 1, cot.astype(F32), 0.0).astype(BF)
        outs = [mm(normed, w_ref[piece], 1, 0).astype(BF) for piece in range(3)]
        outs.append(mm(masked, wo_ref[...], 1, 1).astype(BF))
        return mean, inverse, normed, masked, outs

    def project_rows(i, carry):
        r = pl.multiple_of(i * block, block)
        mean, inverse, normed, masked, outs = project(
            x_ref[pl.ds(r, block), :].astype(F32),
            cot_ref[pl.ds(r, block), :],
            query_ref[pl.ds(r + HALO, block), 1:2],
        )
        centre[pl.ds(r, block), 0:1] = mean
        centre[pl.ds(r, block), 1:2] = inverse
        normed_t[:, pl.ds(r, block)] = normed.T
        masked_t[:, pl.ds(r, block)] = masked.T
        for ext, out in zip((qe, ke, ve, ge), outs):
            ext[pl.ds(r + TILE, block), :] = out
        return carry

    lax.fori_loop(0, rows // block, project_rows, 0)
    for item in halos:
        item.wait_recv()
    at_row = lax.broadcasted_iota(jnp.int32, (2 * HALO, 1), 0)
    inside = jnp.where(
        at_row < HALO,
        jnp.where(tm_at > 0, 1, 0),
        jnp.where(tm_at < tm_count - 1, 1, 0),
    )
    live = jnp.concatenate(
        [query_ref[0:HALO, 1:2], query_ref[HALO + rows : 2 * HALO + rows, 1:2]]
    )
    outs = project(
        jnp.where(inside == 1, halo_x[...].astype(F32), 0.0), halo_cot[...], live
    )[-1]
    for ext, out in zip((qe, ke, ve, ge), outs):
        ext[TILE - HALO : TILE] = out[:HALO]
        ext[edge : edge + HALO] = out[HALO:]

    dka[...] = jnp.zeros_like(dka)
    dva[...] = jnp.zeros_like(dva)
    scale = HS ** (-0.5)
    a = lax.broadcasted_iota(jnp.int32, (TILE, 2 * TILE), 0) + HALO
    b = lax.broadcasted_iota(jnp.int32, (TILE, 2 * TILE), 1)
    apart = a // CH - b // CH
    band = (apart >= -1) & (apart <= 1)
    diagonal = a == b

    def attend(group, lo, hi):
        def tile(t, carry):
            k0 = pl.multiple_of(t * TILE, TILE)
            q0 = pl.multiple_of(t * TILE + HALO, HALO)
            allowed = band & (
                diagonal | (query_ref[pl.ds(k0, TILE), 0:1] == kcode_ref[t])
            )
            for h in range(group * group_cols // HS, (group + 1) * group_cols // HS):
                sl = slice(h * HS, (h + 1) * HS)
                q = qe[pl.ds(q0, TILE), sl]
                g = ge[pl.ds(q0, TILE), sl]
                k = ke[pl.ds(k0, 2 * TILE), sl]
                v = ve[pl.ds(k0, 2 * TILE), sl]
                scores = jnp.where(allowed, mm(q, k, 1, 1) * scale, -1e30)
                weights = jnp.exp(scores - jnp.max(scores, axis=-1, keepdims=True))
                p = weights * (1.0 / jnp.sum(weights, axis=-1, keepdims=True))
                pb = p.astype(BF)
                dp = mm(g, v, 1, 1)
                delta = jnp.sum(p * dp, axis=-1, keepdims=True)
                ds = (p * (dp - delta) * scale).astype(BF)
                oe[pl.ds(q0, TILE), sl] = mm(pb, v, 1, 0).astype(BF)
                dqe[pl.ds(q0, TILE), sl] = mm(ds, k, 1, 0).astype(BF)
                dka[pl.ds(k0, 2 * TILE), sl] += mm(ds, q, 0, 0)
                dva[pl.ds(k0, 2 * TILE), sl] += mm(pb, g, 0, 0)
            return carry

        def three(i, carry):
            for j in range(3):
                tile(lo + 3 * i + j, carry)
            return carry

        whole = (hi - lo) // 3
        lax.fori_loop(0, whole, three, 0)
        lax.fori_loop(lo + 3 * whole, hi, tile, 0)

    def close(group):
        sl = slice(group * group_cols, (group + 1) * group_cols)
        dkb[:, sl] = dka[TILE:edge, sl].astype(BF)
        dvb[:, sl] = dva[TILE:edge, sl].astype(BF)

    def copy(unit, b):
        return pltpu.make_async_remote_copy(
            src_ref=lists[b].at[unit, :, 1 - bits[b]],
            dst_ref=arrivals[b].at[unit],
            send_sem=send_sem.at[unit, b],
            recv_sem=recv_sem.at[unit, b],
            device_id={"tm": partners[b]},
            device_id_type=pl.DeviceIdType.MESH,
        )

    copies = {}
    progress = {}
    step = 256

    def terms(unit):
        group, half = unit // 2, unit % 2
        sl = slice(group * group_cols, (group + 1) * group_cols)
        pairs = (
            ((normed_t, dqe[TILE:edge, sl]), (normed_t, dkb[:, sl]))
            if half == 0
            else ((normed_t, dvb[:, sl]), (masked_t, oe[TILE:edge, sl]))
        )
        for at in range(0, depth, step):
            for side, (left, right) in enumerate(pairs):
                part = mm(left[at : at + step], right, 1, 0).astype(BF)
                for r in range(0, step, chunk):
                    owner = (at + r) // chunk
                    lists[0][unit, owner // 2, owner % 2, :,
                             side * group_cols : (side + 1) * group_cols] = part[r : r + chunk]
        copies[unit, 0] = copy(unit, 0)
        copies[unit, 0].start()
        progress[unit] = 0

    def advance(unit):
        b = progress[unit]
        copies[unit, b].wait_recv()
        if b < phases - 1:
            for j in range(tm_count >> (b + 1)):
                kept = lists[b][unit, j, bits[b]].astype(F32) + arrivals[b][unit, j].astype(F32)
                lists[b + 1][unit, j // 2, j % 2] = kept.astype(BF)
            copies[unit, b + 1] = copy(unit, b + 1)
            copies[unit, b + 1].start()
        else:
            kept = lists[b][unit, 0, bits[b]].astype(F32) + arrivals[b][unit, 0].astype(F32)
            group, half = unit // 2, unit % 2
            sl = slice(group * group_cols, (group + 1) * group_cols)
            first, second = kept[:, :group_cols], kept[:, group_cols:]
            if half == 0:
                qkv_ref[0, :, sl] = first
                qkv_ref[1, :, sl] = second
            else:
                qkv_ref[2, :, sl] = first
                out_ref[sl, :] = second.T
        progress[unit] = b + 1

    def incoming(target, r):
        lane = pl.multiple_of(target * share, 128)
        span = pl.ds(lane, share)
        total = mm(dqe[TILE + r : TILE + r + block], w_ref[0, span, :], 1, 1)
        total += mm(dkb[r : r + block], w_ref[1, span, :], 1, 1)
        total += mm(dvb[r : r + block], w_ref[2, span, :], 1, 1)
        xhat = (x_ref[r : r + block, span].astype(F32) - centre[r : r + block, 0:1]) * centre[
            r : r + block, 1:2
        ]
        scaled = total * gain_ref[:, span]
        first = jnp.sum(scaled, axis=-1, keepdims=True)
        second = jnp.sum(scaled * xhat, axis=-1, keepdims=True)
        return total, first, second

    shares = {}

    def away_shares():
        for s, target in enumerate(mp_targets):
            for i, r in enumerate(range(0, rows, block)):
                total, first, second = incoming(target, r)
                away[s, r : r + block] = total.astype(BF)
                shares[s, i] = pltpu.make_async_remote_copy(
                    src_ref=away.at[s, pl.ds(r, block)],
                    dst_ref=landed.at[s, pl.ds(r, block)],
                    send_sem=share_send.at[s, i],
                    recv_sem=share_recv.at[s, i],
                    device_id={"mp": target},
                    device_id_type=pl.DeviceIdType.MESH,
                )
                shares[s, i].start()
                if s == 0:
                    stats[r : r + block, 0:1] = first
                    stats[r : r + block, 1:2] = second
                else:
                    stats[r : r + block, 0:1] += first
                    stats[r : r + block, 1:2] += second

    def own_share():
        for r in range(0, rows, block):
            total, first, second = incoming(mp_at, r)
            own[r : r + block] = total
            if mp_count > 1:
                first += stats[r : r + block, 0:1]
                second += stats[r : r + block, 1:2]
            lane = lax.broadcasted_iota(jnp.int32, (block, 128), 1)
            both = jnp.where(lane == 0, first, second)
            sums_away[:, r : r + block] = both.T[0:8]
        for s, target in enumerate(mp_targets):
            shares[s, -1] = pltpu.make_async_remote_copy(
                src_ref=sums_away,
                dst_ref=sums_landed.at[s],
                send_sem=sums_send.at[s],
                recv_sem=sums_recv.at[s],
                device_id={"mp": target},
                device_id_type=pl.DeviceIdType.MESH,
            )
            shares[s, -1].start()

    def norm_rows():
        span = pl.ds(pl.multiple_of(mp_at * share, 128), share)
        for s in range(mp_count - 1):
            shares[s, -1].wait_recv()
        for i, r in enumerate(range(0, rows, block)):
            total = own[r : r + block]
            both = sums_away[:, r : r + block]
            for s in range(mp_count - 1):
                shares[s, i].wait_recv()
                total += landed[s, r : r + block].astype(F32)
                both += sums_landed[s, :, r : r + block]
            both = both.T * (1.0 / depth)
            inverse = centre[r : r + block, 1:2]
            xhat = (x_ref[r : r + block, span].astype(F32) - centre[r : r + block, 0:1]) * inverse
            scaled = total * gain_ref[:, span]
            frame_ref[r : r + block] = (
                inverse * (scaled - both[:, 0:1] - xhat * both[:, 1:2])
            ).astype(BF)

    tiles = rows // TILE + 1
    for group in range(groups - 1):
        if group == 0:
            attend(group, 0, tiles)
        close(group)
        terms(2 * group)
        terms(2 * group + 1)
        advance(2 * group)
        third = tiles // 3
        attend(group + 1, 0, third)
        advance(2 * group + 1)
        attend(group + 1, third, 2 * third)
        if phases > 1:
            advance(2 * group)
        attend(group + 1, 2 * third, tiles)
        if phases > 1:
            advance(2 * group + 1)
    if groups == 1:
        attend(0, 0, tiles)
    close(groups - 1)
    away_shares()
    terms(2 * groups - 2)
    terms(2 * groups - 1)
    advance(2 * groups - 2)
    own_share()
    for b in range(phases):
        for unit in range(2 * groups):
            if progress[unit] == b:
                advance(unit)
    norm_rows()
    for item in halos:
        item.wait_send()
    for unit in range(2 * groups):
        for b in range(phases):
            copies[unit, b].wait_send()
    for item in shares.values():
        item.wait_send()


def backward(query, kcode, frames, cot, gain, w, wo, tm_count, mp_count):
    rows, depth = frames.shape
    cols = w.shape[2]
    ext = rows + 2 * TILE
    share = depth // mp_count
    chunk = depth // tm_count
    group_cols = min(cols, 2 * HS)
    units = 2 * (cols // group_cols)
    width = 2 * group_cols
    block = min(rows, 256)
    blocks = rows // block
    peers = max(mp_count - 1, 1)
    phases = tm_count.bit_length() - 1
    vmem = pl.BlockSpec(memory_space=pltpu.VMEM)
    dma = pltpu.SemaphoreType.DMA
    return pl.pallas_call(
        functools.partial(backward_kernel, tm_count, mp_count, group_cols, block),
        name="backward",
        in_specs=[vmem] * 7,
        out_specs=[vmem] * 3,
        out_shape=[
            jax.ShapeDtypeStruct((rows, share), BF),
            jax.ShapeDtypeStruct((3, chunk, cols), F32),
            jax.ShapeDtypeStruct((cols, chunk), F32),
        ],
        scratch_shapes=[pltpu.VMEM((2 * HALO, depth), BF)] * 2
        + [pltpu.VMEM((depth, rows), BF)] * 2
        + [dma((4,))] * 2
        + [pltpu.VMEM((ext, cols), BF)] * 6
        + [pltpu.VMEM((ext, cols), F32)] * 2
        + [pltpu.VMEM((rows, cols), BF)] * 2
        + [pltpu.VMEM((rows, 2), F32)] * 2
        + [
            pltpu.VMEM((rows, share), F32),
            pltpu.VMEM((peers, rows, share), BF),
            pltpu.VMEM((peers, rows, share), BF),
            pltpu.VMEM((8, rows), F32),
            pltpu.VMEM((peers, 8, rows), F32),
        ]
        + [
            pltpu.VMEM((units, tm_count >> (b + 1), 2, chunk, width), BF) for b in range(phases)
        ]
        + [pltpu.VMEM((units, tm_count >> (b + 1), chunk, width), BF) for b in range(phases)]
        + [
            dma((units, phases)),
            dma((units, phases)),
            dma((peers, blocks)),
            dma((peers, blocks)),
            dma((peers,)),
            dma((peers,)),
        ],
        compiler_params=pltpu.CompilerParams(
            vmem_limit_bytes=VMEM_LIMIT, collective_id=0, has_side_effects=True
        ),
        cost_estimate=pl.CostEstimate(
            flops=24 * rows * depth * cols, bytes_accessed=30 * rows * depth,
            transcendentals=rows * cols,
        ),
    )(query, kcode, frames, cot, gain, w, wo)


def on_device(frames, norm_gain, qkv_weight, out_weight, cotangent, pad_mask, utt_lengths):
    rows = frames.shape[0]
    tm_count = lax.axis_size("tm")
    mp_count = lax.axis_size("mp")
    first_row = lax.axis_index("tm") * rows
    gain = norm_gain[None, :]

    ext = rows + 2 * TILE
    positions = first_row - TILE + jnp.arange(ext, dtype=jnp.int32)
    ends = jnp.cumsum(utt_lengths)
    segment = jnp.sum((ends[:, None] <= positions[None, :]).astype(jnp.int32), axis=0)
    live = lax.dynamic_slice(jnp.pad(pad_mask, TILE), (first_row,), (ext,))
    code = jnp.where(live == 1, segment, -1).reshape(-1, 1, TILE)
    kcode = jnp.concatenate([code[:-1], code[1:]], axis=2)
    query = jnp.stack([segment, live], axis=1)[HALO : ext - HALO]
    return tuple(
        backward(
            query, kcode, frames, cotangent, gain, qkv_weight, out_weight, tm_count, mp_count
        )
    )


def solution(mesh):
    placed = (
        P(("batch", "tm"), None),
        P(),
        P(None, None, "mp"),
        P("mp", None),
        P(("batch", "tm"), None),
        P("batch"),
        P("batch"),
    )
    return jax.shard_map(
        on_device,
        mesh=mesh,
        in_specs=placed,
        out_specs=(P(("batch", "tm"), "mp"), P("batch", "tm", "mp"), P(("batch", "mp"), "tm")),
        check_vma=False,
    )
```
